32 devices in a mesh: occ: 4 (over z), va: 2 (over x), vb: 4 (over y, core).
Axes of the slice: x: 2, y: 2, z: 4, core: 2. Of those that a mesh axis runs over, the one named last changes fastest.
Arguments:
- aux_factors: bfloat16 [4, 1024, 2048], P('occ', ('vb', 'va')), may hold values from -0.59765625 to 0.59765625
- occ_energy: float32 [4], replicated, may hold values from -2 to -0.5
- vir_energy: float32 [1024], replicated, may hold values from 0.5 to 3
- occ_index: int32 [4], replicated, may hold values from 0 to 3, each once
- vir_index: int32 [1024], replicated, may hold values from 0 to 1023, each once
Outputs:
- gamma_aux: float32 [4, 1024, 2048], P('occ', ('vb', 'va'))
The draws below stay inside these ranges and needn't reach their ends.
Inputs may be any that keep to these rules, and one draw needn't show every extreme that they name: `occ_index`: each occupied table row appears exactly once. `vir_index`: each virtual table row appears exactly once.
All inputs are finite; a program needn't handle non-finite values.
Results may differ from the reference program's by a relative error of at most 0.0017.
Values may be sent and summed in bfloat16 or wider, within the bound.
No kernel may reach another device: no remote copies, remote signals or barrier semaphores. Data moves between devices by JAX's collectives and lax.ppermute only.
A program may use at most 64 MiB of HBM per device.

```python
import jax
import jax.numpy as jnp
from jax import lax

V = 1024
NAUX = 2048
O_DEV = 1
STEPS = 4
O = 4


def level_of(rng, dims, cuts, low, largest):
    level = 1.0
    for axis_at, parts in cuts:
        draws = jax.random.uniform(jax.random.fold_in(jax.random.fold_in(rng, 6), axis_at), (parts,), jnp.float32, low / len(cuts), largest / len(cuts))
        level = level * jnp.repeat(jnp.exp(draws), dims[axis_at] // parts).reshape((-1,) + (1,) * (len(dims) - 1 - axis_at))
    return level


def bell_draw(rng, dims, width, reach, pieces=(), kind=jnp.bfloat16):
    drawn = jax.random.normal(rng, dims, jnp.float32) * width
    if len(pieces) > 0:
        drawn = level_of(rng, dims, pieces, -0.22, 0.18) * drawn
    return jnp.clip(drawn, min=-reach, max=reach).astype(kind)


def setup_inputs(seed: int = 0) -> dict:
    streams_of = jax.random.split(jax.random.key(seed), 6)
    return {
        "aux_factors": bell_draw(streams_of[0], (O, V, NAUX), 0.1, 0.59765625, ((0, 4), (1, 8))),
        "occ_energy": jnp.clip(jax.random.uniform(streams_of[1], (O,), jnp.float32, -2.0, -0.5), -2.0, -0.5),
        "vir_energy": jnp.clip(jax.random.uniform(streams_of[2], (V,), jnp.float32, 0.5, 3.0), 0.5, 3.0),
        "occ_index": jax.random.permutation(streams_of[3], O).astype(jnp.int32),
        "vir_index": jax.random.permutation(streams_of[4], V).astype(jnp.int32),
    }


def pair_term(resident, partner, eps_left, eps_right, eps_vir):
    kernel = jnp.einsum("iap,jbp->iajb", resident.astype(jnp.float32), partner.astype(jnp.float32))
    swapped = jnp.transpose(kernel, (0, 3, 2, 1))
    energy_gap = (eps_left[:, None, None, None] + eps_right[None, None, :, None]
                  - eps_vir[None, :, None, None] - eps_vir[None, None, None, :])
    weights = ((2.0 * kernel - swapped) / energy_gap).astype(jnp.bfloat16)
    return jnp.einsum("iajb,jbp->iap", weights.astype(jnp.float32), partner.astype(jnp.float32))


def reference(aux_factors, occ_energy, vir_energy, occ_index, vir_index):
    blocks_count = O // O_DEV
    eps_occ = occ_energy[occ_index].reshape(blocks_count, O_DEV)
    eps_vir = vir_energy[vir_index]
    blocks = aux_factors.reshape(blocks_count, O_DEV, V, NAUX)

    def one_block(home_block):
        resident = lax.dynamic_index_in_dim(blocks, home_block, 0, False)
        eps_left = lax.dynamic_index_in_dim(eps_occ, home_block, 0, False)
        accumulated = jnp.zeros((O_DEV, V, NAUX), jnp.float32)
        for distance in range(STEPS):
            other_block = (home_block - distance + blocks_count) % blocks_count
            partner = lax.dynamic_index_in_dim(blocks, other_block, 0, False)
            eps_right = lax.dynamic_index_in_dim(eps_occ, other_block, 0, False)
            accumulated = accumulated + pair_term(resident, partner, eps_left, eps_right, eps_vir)
        return accumulated

    result = lax.map(one_block, jnp.arange(blocks_count, dtype=jnp.int32))
    return result.reshape(O, V, NAUX)
```

```python
import functools

import jax
import jax.numpy as jnp
from jax import lax
from jax.experimental import pallas as pl
from jax.experimental.pallas import tpu as pltpu
from jax.sharding import PartitionSpec as P

STEPS = 4
CORES = 2

NT = (((1,), (1,)), ((), ()))


def lookup(indices, energies):
    positions = jnp.arange(energies.shape[0], dtype=jnp.int32)
    matches = indices[:, None] == positions[None, :]
    return jnp.sum(jnp.where(matches, energies[None, :], 0.0), axis=1)


def contract(blocks, planes, labels, first, *refs):
    refs = list(refs)
    pair_energy = refs.pop(0)
    row_energy = refs.pop(0)
    col_energy = refs.pop(0)
    rows = [refs.pop(0), refs.pop(0)]
    near = {p: refs.pop(0) for p in planes}
    far_rows = {d: [refs.pop(0), refs.pop(0)] for d in labels}
    far = [refs.pop(0) for _ in blocks]
    sums_in = None if first else [refs.pop(0), refs.pop(0)]
    sums_out = refs
    count = rows[0].shape[0]
    own = jnp.concatenate([r[...] for r in rows], axis=0)
    weights = []
    for (p, d), block in zip(blocks, far):
        there = jnp.concatenate([r[...] for r in far_rows[d]], axis=0)
        direct = lax.dot_general(own, block[...], NT, preferred_element_type=jnp.float32)
        swapped = lax.dot_general(there, near[p][...], NT, preferred_element_type=jnp.float32)
        gap = pair_energy[d] - row_energy[...] - col_energy[pl.ds(p, 1), :]
        weights.append(((2.0 * direct - swapped) / gap).astype(jnp.bfloat16))
    weights = jnp.concatenate(weights, axis=1)
    columns = jnp.concatenate([b[...] for b in far], axis=0)
    for half in range(CORES):
        part = jnp.dot(
            weights[half * count : (half + 1) * count], columns, preferred_element_type=jnp.float32
        )
        sums_out[half][...] = part if first else sums_in[half][...] + part


def per_device(aux_factors, occ_energy, vir_energy, occ_index, vir_index):
    va_count = lax.axis_size("va")
    vb_count = lax.axis_size("vb")
    occ_count = lax.axis_size("occ")
    chip_count = vb_count // CORES
    occ_rows, width, aux_width = aux_factors.shape
    assert occ_rows == 1 and vb_count % CORES == 0
    paired = occ_count == STEPS and STEPS & (STEPS - 1) == 0

    def from_va(block, step):
        return lax.ppermute(block, "va", [((i - step) % va_count, i) for i in range(va_count)])

    def from_vb(block, step):
        move = step * CORES
        return lax.ppermute(block, "vb", [((i - move) % vb_count, i) for i in range(vb_count)])

    def from_core(block):
        return lax.ppermute(block, "vb", [(i ^ 1, i) for i in range(vb_count)])

    def partner(i, step):
        return i ^ step if paired else (i - step) % occ_count

    def from_occ(block, step):
        return lax.ppermute(block, "occ", [(partner(i, step), i) for i in range(occ_count)])

    own = aux_factors[0]
    line = {0: own}
    for d in range(1, STEPS):
        low = d & -d
        line[d] = from_occ(line[d - low], low)
    other = {d: from_core(line[d]) for d in range(STEPS)}
    plane_of = {(dx, dy): dx * chip_count + dy for dx in range(va_count) for dy in range(chip_count)}
    held = {}
    for d in range(STEPS):
        for (dx, dy), p in plane_of.items():
            if dx == 0 and dy == 0:
                held[p, d] = line[d]
            elif dy == 0:
                held[p, d] = from_va(line[d], dx)
            elif dx == 0:
                held[p, d] = from_vb(line[d], dy)
    for d in range(STEPS):
        for (dx, dy), p in plane_of.items():
            if dx > 0 and dy > 0:
                if d == 1:
                    held[p, d] = from_occ(held[p, 0], 1)
                elif d % 2 == 0:
                    held[p, d] = from_va(held[plane_of[0, dy], d], dx)
                else:
                    held[p, d] = from_vb(held[plane_of[dx, 0], d], dy)

    va_rank = lax.axis_index("va")
    vb_rank = lax.axis_index("vb")
    occ_rank = lax.axis_index("occ")
    eps_v = lookup(vir_index, vir_energy).reshape(vb_count * va_count, width)
    eps_o = lookup(occ_index, occ_energy)
    core = vb_rank % CORES
    chip = vb_rank // CORES

    def energies(dx, dy, flip):
        vb = (chip - dy) % chip_count * CORES + (core ^ flip)
        return lax.dynamic_index_in_dim(eps_v, vb * va_count + (va_rank - dx) % va_count, 0, False)

    row_energy = jnp.concatenate([energies(0, 0, 0), energies(0, 0, 1)])
    row_energy = jnp.broadcast_to(row_energy[:, None], (CORES * width, width))
    col_energy = jnp.stack([energies(dx, dy, 0) for dx, dy in plane_of])
    far_ids = [partner(occ_rank, d) for d in range(STEPS)]
    pair_energy = jnp.stack([eps_o[occ_rank] + eps_o[far] for far in far_ids])

    whole = pl.BlockSpec(memory_space=pltpu.VMEM)
    scalar = pl.BlockSpec(memory_space=pltpu.SMEM)
    total = jax.ShapeDtypeStruct((width, aux_width), jnp.float32)
    sums = None

    def add(blocks, sums):
        planes = sorted({p for p, _ in blocks})
        labels = sorted({d for _, d in blocks})
        operands = [pair_energy, row_energy, col_energy, own, other[0]]
        operands += [held[p, 0] for p in planes]
        for d in labels:
            operands += [line[d], other[d]]
        operands += [held[b] for b in blocks]
        aliases = {}
        if sums is not None:
            aliases = {len(operands) + k: k for k in range(CORES)}
            operands += list(sums)
        flops = 2 * 3 * len(blocks) * CORES * width * width * aux_width
        return pl.pallas_call(
            functools.partial(contract, blocks, planes, labels, sums is None),
            out_shape=(total, total),
            in_specs=[scalar] + [whole] * (len(operands) - 1),
            out_specs=(whole, whole),
            input_output_aliases=aliases,
            cost_estimate=pl.CostEstimate(
                flops=flops, bytes_accessed=len(blocks) * width * aux_width * 4, transcendentals=0
            ),
            compiler_params=pltpu.CompilerParams(vmem_limit_bytes=24 << 20),
        )(*operands)

    crossed = [p for (dx, dy), p in plane_of.items() if dx > 0 and dy > 0]
    straight = [p for p in plane_of.values() if p not in crossed]
    groups = [[(p, 0) for p in straight + crossed]]
    groups += [[(p, d) for p in straight] for d in range(1, STEPS)]
    groups[-1] += [(p, 1) for p in crossed]
    groups.append([(p, d) for d in range(2, STEPS) for p in crossed])
    for blocks in groups:
        sums = add(blocks, sums)
    return (sums[0] + from_core(sums[1]))[None]


def solution(mesh):
    return jax.shard_map(
        per_device,
        mesh=mesh,
        in_specs=(P("occ", ("vb", "va"), None), P(), P(), P(), P()),
        out_specs=P("occ", ("vb", "va"), None),
        check_vma=False,
    )
```

```python
import functools

import jax
import jax.numpy as jnp
from jax import lax
from jax.experimental import pallas as pl
from jax.experimental.pallas import tpu as pltpu
from jax.sharding import PartitionSpec as P


STEPS = 4
CORES = 2

NT = (((1,), (1,)), ((), ()))


def prepare(sizes, partner, index_ref, vir_ref, occ_index_ref, occ_ref, pair_ref, row_ref, col_ref):
    va_count, chip_count, occ_count = sizes
    va, vb, occ = lax.axis_index("va"), lax.axis_index("vb"), lax.axis_index("occ")
    core, chip = lax.rem(vb, CORES), vb // CORES
    index = index_ref[...]
    width = index.shape[1]

    def step(k, found):
        return found + jnp.where(index == k, vir_ref[k], 0.0)

    energy = lax.fori_loop(
        0, vir_ref.shape[0], step, jnp.zeros(index.shape, jnp.float32), unroll=16
    )

    def block(dx, dy, flip):
        other = lax.rem(chip - dy + chip_count, chip_count) * CORES + lax.rem(core + flip, CORES)
        mine = other * va_count + lax.rem(va - dx + va_count, va_count)
        picked = lax.broadcasted_iota(jnp.int32, index.shape, 0) == mine
        return jnp.sum(jnp.where(picked, energy, 0.0), axis=0, keepdims=True)

    for flip in range(CORES):
        spread = jnp.broadcast_to(block(0, 0, flip), (width, width))
        row_ref[flip * width : (flip + 1) * width, :] = jnp.transpose(spread)
    for dx in range(va_count):
        for dy in range(chip_count):
            p = dx * chip_count + dy
            col_ref[p : p + 1, :] = block(dx, dy, 0)
    for d in range(STEPS):
        far = partner(occ, d, occ_count)
        pair_ref[d] = occ_ref[occ_index_ref[occ]] + occ_ref[occ_index_ref[far]]


def contract(blocks, first, *refs):
    refs = list(refs)
    pair_energy, row_energy, col_energy = (refs.pop(0) for _ in range(3))
    rows = [refs.pop(0), refs.pop(0)]
    near = {p: refs.pop(0) for p in sorted({p for d, ps in blocks for p in ps if d > 0})}
    far_rows = {d: [refs.pop(0), refs.pop(0)] for d, _ in blocks if d > 0}
    far = {(d, p): refs.pop(0) for d, ps in blocks for p in ps}
    sums_in = None if first else [refs.pop(0), refs.pop(0)]
    sums_out = refs
    count = rows[0].shape[0]

    def stack(parts):
        return jnp.concatenate([r[...] for r in parts], axis=0)

    own = stack(rows)
    weights = []
    for d, ps in blocks:
        direct = lax.dot_general(
            own, stack([far[d, p] for p in ps]), NT, preferred_element_type=jnp.float32
        )
        if d > 0:
            swapped = lax.dot_general(
                stack(far_rows[d]), stack([near[p] for p in ps]), NT,
                preferred_element_type=jnp.float32,
            )
        else:
            swapped = direct
        for k, p in enumerate(ps):
            cut = slice(k * count, (k + 1) * count)
            gap = pair_energy[d] - row_energy[...] - col_energy[p : p + 1, :]
            weights.append(((2.0 * direct[:, cut] - swapped[:, cut]) / gap).astype(jnp.bfloat16))
    weights = jnp.concatenate(weights, axis=1)
    columns = stack([far[d, p] for d, ps in blocks for p in ps])
    for half in range(CORES):
        part = jnp.dot(
            weights[half * count : (half + 1) * count], columns, preferred_element_type=jnp.float32
        )
        sums_out[half][...] = part if first else sums_in[half][...] + part


def per_device(aux_factors, occ_energy, vir_energy, occ_index, vir_index):
    va_count = lax.axis_size("va")
    vb_count = lax.axis_size("vb")
    occ_count = lax.axis_size("occ")
    chip_count = vb_count // CORES
    occ_rows, width, aux_width = aux_factors.shape
    assert occ_rows == 1 and vb_count % CORES == 0
    paired = occ_count == STEPS and STEPS & (STEPS - 1) == 0

    def partner(i, step, count):
        return i ^ step if paired else (i + count - step) % count

    def from_va(block, step):
        return lax.ppermute(block, "va", [((i - step) % va_count, i) for i in range(va_count)])

    def from_vb(block, step):
        move = step * CORES
        return lax.ppermute(block, "vb", [((i - move) % vb_count, i) for i in range(vb_count)])

    def from_core(block):
        return lax.ppermute(block, "vb", [(i ^ 1, i) for i in range(vb_count)])

    def from_occ(block, step):
        return lax.ppermute(
            block, "occ", [(partner(i, step, occ_count), i) for i in range(occ_count)]
        )

    own = aux_factors[0]
    line = {0: own}
    for d in range(1, STEPS):
        low = d & -d
        line[d] = from_occ(line[d - low], low)
    other = {d: from_core(line[d]) for d in range(STEPS)}
    plane_of = {(dx, dy): dx * chip_count + dy for dx in range(va_count) for dy in range(chip_count)}
    held = {}
    for d in range(STEPS):
        for (dx, dy), p in plane_of.items():
            if dx == 0 and dy == 0:
                held[d, p] = line[d]
            elif dy == 0:
                held[d, p] = from_va(line[d], dx)
            elif dx == 0:
                held[d, p] = from_vb(line[d], dy)
    for d in range(STEPS):
        for (dx, dy), p in plane_of.items():
            if dx > 0 and dy > 0:
                if d % 2 == 1:
                    held[d, p] = from_occ(held[d - 1, p], 1)
                elif d == 0:
                    held[d, p] = from_va(held[d, plane_of[0, dy]], dx)
                else:
                    held[d, p] = from_vb(held[d, plane_of[dx, 0]], dy)

    whole = pl.BlockSpec(memory_space=pltpu.VMEM)
    scalar = pl.BlockSpec(memory_space=pltpu.SMEM)
    f32 = jnp.float32

    def energies():
        return pl.pallas_call(
            functools.partial(prepare, (va_count, chip_count, occ_count), partner),
            out_shape=(
                jax.ShapeDtypeStruct((STEPS,), f32),
                jax.ShapeDtypeStruct((CORES * width, width), f32),
                jax.ShapeDtypeStruct((len(plane_of), width), f32),
            ),
            in_specs=[whole, scalar, scalar, scalar],
            out_specs=(scalar, whole, whole),
            cost_estimate=pl.CostEstimate(
                flops=3 * vir_index.shape[0] ** 2, bytes_accessed=1 << 18, transcendentals=0
            ),
        )(vir_index.reshape(-1, width), vir_energy, occ_index, occ_energy)

    tables = energies()
    total = jax.ShapeDtypeStruct((width, aux_width), f32)

    def add(blocks, sums):
        operands = [*tables, own, other[0]]
        operands += [held[0, p] for p in sorted({p for d, ps in blocks for p in ps if d > 0})]
        for d, _ in blocks:
            operands += [line[d], other[d]] if d > 0 else []
        operands += [held[d, p] for d, ps in blocks for p in ps]
        aliases = {}
        if sums is not None:
            aliases = {len(operands) + k: k for k in range(CORES)}
            operands += list(sums)
        count = sum(len(ps) for _, ps in blocks)
        return pl.pallas_call(
            functools.partial(contract, blocks, sums is None),
            out_shape=(total, total),
            in_specs=[scalar] + [whole] * (len(operands) - 1),
            out_specs=(whole, whole),
            input_output_aliases=aliases,
            cost_estimate=pl.CostEstimate(
                flops=2 * 3 * count * CORES * width * width * aux_width,
                bytes_accessed=count * width * aux_width * 4,
                transcendentals=0,
            ),
            compiler_params=pltpu.CompilerParams(vmem_limit_bytes=24 << 20),
        )(*operands)

    here = [plane_of[0, 0]]
    xs = [p for (dx, dy), p in plane_of.items() if dx > 0 and dy == 0]
    ys = [p for (dx, dy), p in plane_of.items() if dx == 0 and dy > 0]
    cs = [p for (dx, dy), p in plane_of.items() if dx > 0 and dy > 0]
    groups = (
        ((0, here + xs + ys + cs),),
        ((1, here + ys), (2, here + xs + ys)),
        ((1, xs + cs), (2, cs), (3, here)),
        ((3, xs + ys + cs),),
    )
    sums = None
    for blocks in groups:
        sums = add(blocks, sums)
    return (sums[0] + from_core(sums[1]))[None]


def solution(mesh):
    return jax.shard_map(
        per_device,
        mesh=mesh,
        in_specs=(P("occ", ("vb", "va"), None), P(), P(), P(), P()),
        out_specs=P("occ", ("vb", "va"), None),
        check_vma=False,
    )
```

```python
import functools

import jax
import jax.numpy as jnp
from jax import lax
from jax.experimental import pallas as pl
from jax.experimental.pallas import tpu as pltpu
from jax.sharding import PartitionSpec as P


STEPS = 4
CORES = 2

NT = (((1,), (1,)), ((), ()))


def prepare(sizes, partner, index_ref, vir_ref, occ_index_ref, occ_ref, pair_ref, row_ref, col_ref):
    va_count, chip_count, occ_count = sizes
    va, vb, occ = lax.axis_index("va"), lax.axis_index("vb"), lax.axis_index("occ")
    core, chip = lax.rem(vb, CORES), vb // CORES
    index = index_ref[...]
    width = index.shape[1]

    lanes = 8
    share = vir_ref.shape[0] // lanes

    def step(k, found):
        return tuple(
            f + jnp.where(index == n * share + k, vir_ref[n * share + k], 0.0)
            for n, f in enumerate(found)
        )

    zero = jnp.zeros(index.shape, jnp.float32)
    found = lax.fori_loop(0, share, step, (zero,) * lanes, unroll=4)
    energy = sum(found[1:], found[0])

    def block(dx, dy, flip):
        other = lax.rem(chip - dy + chip_count, chip_count) * CORES + lax.rem(core + flip, CORES)
        mine = other * va_count + lax.rem(va - dx + va_count, va_count)
        picked = lax.broadcasted_iota(jnp.int32, index.shape, 0) == mine
        return jnp.sum(jnp.where(picked, energy, 0.0), axis=0, keepdims=True)

    for flip in range(CORES):
        spread = jnp.broadcast_to(block(0, 0, flip), (width, width))
        row_ref[flip * width : (flip + 1) * width, :] = jnp.transpose(spread)
    for dx in range(va_count):
        for dy in range(chip_count):
            for flip in range(CORES):
                p = (flip * va_count + dx) * chip_count + dy
                col_ref[p : p + 1, :] = block(dx, dy, flip)
    for d in range(STEPS):
        far = partner(occ, d, occ_count)
        pair_ref[d] = occ_ref[occ_index_ref[occ]] + occ_ref[occ_index_ref[far]]


def needed(blocks):
    return sorted({p for d, ps in blocks for p in ps if d > 0})


def contract(blocks, parts, first, *refs):
    refs = list(refs)
    pair_energy, row_energy, col_energy = (refs.pop(0) for _ in range(3))
    rows = [refs.pop(0), refs.pop(0)]
    near = {p: [refs.pop(0) for _ in range(parts[0, p])] for p in needed(blocks)}
    far_rows = {d: [refs.pop(0), refs.pop(0)] for d, _ in blocks if d > 0}
    far = {(d, p): [refs.pop(0) for _ in range(parts[d, p])] for d, ps in blocks for p in ps}
    sums_in = None if first else [refs.pop(0), refs.pop(0)]
    sums_out = refs
    count = rows[0].shape[0]

    def stack(parts):
        return jnp.concatenate([r[...] for r in parts], axis=0)

    own = stack(rows)
    weights = []
    for d, ps in blocks:
        direct = lax.dot_general(
            own, stack([r for p in ps for r in far[d, p]]), NT, preferred_element_type=jnp.float32
        )
        if d > 0:
            swapped = lax.dot_general(
                stack(far_rows[d]), stack([r for p in ps for r in near[p]]), NT,
                preferred_element_type=jnp.float32,
            )
        else:
            swapped = direct
        for k, p in enumerate(ps):
            cut = slice(k * count, (k + 1) * count)
            gap = pair_energy[d] - row_energy[...] - col_energy[p : p + 1, :]
            weights.append(((2.0 * direct[:, cut] - swapped[:, cut]) / gap).astype(jnp.bfloat16))
    weights = jnp.concatenate(weights, axis=1)
    columns = stack([r for d, ps in blocks for p in ps for r in far[d, p]])
    for half in range(CORES):
        part = jnp.dot(
            weights[half * count : (half + 1) * count], columns, preferred_element_type=jnp.float32
        )
        sums_out[half][...] = part if first else sums_in[half][...] + part


def finish(label, cuts, final, *refs):
    refs = list(refs)
    pair_energy, row_energy, col_energy, own, there = (refs.pop(0) for _ in range(5))
    near = [refs.pop(0) for _ in cuts]
    far = [refs.pop(0) for _ in cuts]
    count = own.shape[0]
    columns = jnp.concatenate([r[...] for r in far], axis=0)
    direct = lax.dot_general(own[...], columns, NT, preferred_element_type=jnp.float32)
    swapped = lax.dot_general(
        there[...], jnp.concatenate([r[...] for r in near], axis=0), NT,
        preferred_element_type=jnp.float32,
    )
    table = jnp.concatenate([col_energy[p : p + 1, cut] for p, cut in cuts], axis=1)
    row = jnp.concatenate([row_energy[:count, cut] for _, cut in cuts], axis=1)
    gap = pair_energy[label] - row - table
    weights = ((2.0 * direct - swapped) / gap).astype(jnp.bfloat16)
    if not final:
        sums, out = refs
        out[...] = sums[...] + jnp.dot(weights, columns, preferred_element_type=jnp.float32)
        return
    *sums, out, buffer, sems = refs
    depth = out.shape[1] // sems.shape[0]
    copies = []
    for k in range(sems.shape[0]):
        cut = slice(k * depth, (k + 1) * depth)
        part = jnp.dot(weights, columns[:, cut], preferred_element_type=jnp.float32)
        buffer[:, cut] = (sums[0][:, cut] + sums[1][:, cut]) + part
        copies.append(pltpu.make_async_copy(buffer.at[:, cut], out.at[:, cut], sems.at[k]))
        copies[-1].start()
    for copy in copies:
        copy.wait()


def per_device(aux_factors, occ_energy, vir_energy, occ_index, vir_index):
    va_count = lax.axis_size("va")
    vb_count = lax.axis_size("vb")
    occ_count = lax.axis_size("occ")
    chip_count = vb_count // CORES
    occ_rows, width, aux_width = aux_factors.shape
    assert occ_rows == 1 and vb_count % CORES == 0
    paired = occ_count == STEPS and STEPS & (STEPS - 1) == 0

    def partner(i, step, count):
        return i ^ step if paired else (i + count - step) % count

    def from_va(block, step):
        return lax.ppermute(block, "va", [((i - step) % va_count, i) for i in range(va_count)])

    def from_vb(block, step):
        move = step * CORES
        return lax.ppermute(block, "vb", [((i - move) % vb_count, i) for i in range(vb_count)])

    def from_core(block):
        return lax.ppermute(block, "vb", [(i ^ 1, i) for i in range(vb_count)])

    def from_occ(block, step):
        return lax.ppermute(
            block, "occ", [(partner(i, step, occ_count), i) for i in range(occ_count)]
        )

    own = aux_factors[0]
    line = {0: own}
    for d in range(1, STEPS):
        low = d & -d
        line[d] = from_occ(line[d - low], low)
    other = {d: from_core(line[d]) for d in range(STEPS)}
    plane_of = {(dx, dy): dx * chip_count + dy for dx in range(va_count) for dy in range(chip_count)}
    held = {}
    for d in range(STEPS):
        for (dx, dy), p in plane_of.items():
            if dx == 0 and dy == 0:
                held[d, p] = line[d]
            elif dy == 0:
                held[d, p] = from_va(line[d], dx)
            elif dx == 0:
                held[d, p] = from_vb(line[d], dy)
    held = {key: [block] for key, block in held.items()}
    for d in range(STEPS):
        for (dx, dy), p in plane_of.items():
            if dx > 0 and dy > 0 and d % 2 == 1:
                first, second = held[d - 1, p]
                held[d, p] = [from_occ(first, 1), from_occ(second, 1)]
            elif dx > 0 and dy > 0:
                first = held[d, plane_of[0, dy]][0][: width // 2]
                second = held[d, plane_of[dx, 0]][0][width // 2 :]
                held[d, p] = [from_va(first, dx), from_vb(second, dy)]

    whole = pl.BlockSpec(memory_space=pltpu.VMEM)
    scalar = pl.BlockSpec(memory_space=pltpu.SMEM)
    f32 = jnp.float32

    def energies():
        return pl.pallas_call(
            functools.partial(prepare, (va_count, chip_count, occ_count), partner),
            out_shape=(
                jax.ShapeDtypeStruct((STEPS,), f32),
                jax.ShapeDtypeStruct((CORES * width, width), f32),
                jax.ShapeDtypeStruct((CORES * len(plane_of), width), f32),
            ),
            in_specs=[whole, scalar, scalar, scalar],
            out_specs=(scalar, whole, whole),
            cost_estimate=pl.CostEstimate(
                flops=3 * vir_index.shape[0] ** 2, bytes_accessed=1 << 18, transcendentals=0
            ),
        )(vir_index.reshape(-1, width), vir_energy, occ_index, occ_energy)

    parts = {key: len(pieces) for key, pieces in held.items()}
    tables = energies()
    total = jax.ShapeDtypeStruct((width, aux_width), f32)

    def add(blocks, sums):
        operands = [*tables, own, other[0]]
        operands += [part for p in needed(blocks) for part in held[0, p]]
        for d, _ in blocks:
            operands += [line[d], other[d]] if d > 0 else []
        operands += [part for d, ps in blocks for p in ps for part in held[d, p]]
        aliases = {}
        if sums is not None:
            aliases = {len(operands) + k: k for k in range(CORES)}
            operands += list(sums)
        count = sum(len(ps) for _, ps in blocks)
        return pl.pallas_call(
            functools.partial(contract, blocks, parts, sums is None),
            out_shape=(total, total),
            in_specs=[scalar] + [whole] * (len(operands) - 1),
            out_specs=(whole, whole),
            input_output_aliases=aliases,
            cost_estimate=pl.CostEstimate(
                flops=2 * 3 * count * CORES * width * width * aux_width,
                bytes_accessed=count * width * aux_width * 4,
                transcendentals=0,
            ),
            compiler_params=pltpu.CompilerParams(vmem_limit_bytes=24 << 20),
        )(*operands)

    here = [plane_of[0, 0]]
    xs = [p for (dx, dy), p in plane_of.items() if dx > 0 and dy == 0]
    ys = [p for (dx, dy), p in plane_of.items() if dx == 0 and dy > 0]
    cs = [p for (dx, dy), p in plane_of.items() if dx > 0 and dy > 0]
    groups = (
        ((0, here + xs + ys + cs),),
        ((1, here + xs + ys),),
        ((2, here + xs + ys),),
        ((1, cs), (2, cs), (3, here)),
        ((3, xs + ys),),
    )
    sums = None
    for blocks in groups:
        sums = add(blocks, sums)
    sums = [sums[0], from_core(sums[1])]

    pieces = parts[0, cs[0]]
    swapped = {
        (d, p, k): from_core(held[d, p][k])
        for d in (0, 3)
        for p in cs
        for k in range(pieces)
    }

    def late(k, final, *sums):
        size = width // pieces
        cut = slice(k * size, (k + 1) * size)
        operands = [*tables, own, line[3]]
        for d in (0, 3):
            operands += [held[d, p][k] for p in cs] + [swapped[d, p, k] for p in cs]
        operands += sums
        rows = [core * len(plane_of) + p for core in range(CORES) for p in cs]
        return pl.pallas_call(
            functools.partial(finish, 3, [(row, cut) for row in rows], final),
            out_shape=total,
            in_specs=[scalar] + [whole] * (len(operands) - 1),
            out_specs=pl.BlockSpec(memory_space=pl.ANY) if final else whole,
            scratch_shapes=[pltpu.VMEM(total.shape, f32), pltpu.SemaphoreType.DMA((4,))]
            if final
            else [],
            cost_estimate=pl.CostEstimate(
                flops=2 * 3 * len(rows) * width * size * aux_width,
                bytes_accessed=width * aux_width * 4,
                transcendentals=0,
            ),
            compiler_params=pltpu.CompilerParams(vmem_limit_bytes=16 << 20),
        )(*operands)

    mine = sums[0]
    for k in range(pieces - 1):
        mine = late(k, False, mine)
    return late(pieces - 1, True, mine, sums[1])[None]


def solution(mesh):
    return jax.shard_map(
        per_device,
        mesh=mesh,
        in_specs=(P("occ", ("vb", "va"), None), P(), P(), P(), P()),
        out_specs=P("occ", ("vb", "va"), None),
        check_vma=False,
    )
```

```python
import functools

import jax
import jax.numpy as jnp
from jax import lax
from jax.experimental import pallas as pl
from jax.experimental.pallas import tpu as pltpu
from jax.sharding import PartitionSpec as P


STEPS = 4
CORES = 2

NT = (((1,), (1,)), ((), ()))


def prepare(sizes, partner, index_ref, vir_ref, occ_index_ref, occ_ref, pair_ref, row_ref, col_ref):
    va_count, chip_count, occ_count = sizes
    va, vb, occ = lax.axis_index("va"), lax.axis_index("vb"), lax.axis_index("occ")
    core, chip = lax.rem(vb, CORES), vb // CORES
    index = index_ref[...]
    width = index.shape[1]

    lanes = 8
    share = vir_ref.shape[0] // lanes

    def step(k, found):
        return tuple(
            f + jnp.where(index == n * share + k, vir_ref[n * share + k], 0.0)
            for n, f in enumerate(found)
        )

    zero = jnp.zeros(index.shape, jnp.float32)
    found = lax.fori_loop(0, share, step, (zero,) * lanes, unroll=4)
    energy = sum(found[1:], found[0])

    def block(dx, dy, flip):
        other = lax.rem(chip - dy + chip_count, chip_count) * CORES + lax.rem(core + flip, CORES)
        mine = other * va_count + lax.rem(va - dx + va_count, va_count)
        picked = lax.broadcasted_iota(jnp.int32, index.shape, 0) == mine
        return jnp.sum(jnp.where(picked, energy, 0.0), axis=0, keepdims=True)

    for flip in range(CORES):
        spread = jnp.broadcast_to(block(0, 0, flip), (width, width))
        row_ref[flip * width : (flip + 1) * width, :] = jnp.transpose(spread)
    for dx in range(va_count):
        for dy in range(chip_count):
            for flip in range(CORES):
                p = (flip * va_count + dx) * chip_count + dy
                col_ref[p : p + 1, :] = block(dx, dy, flip)
    for d in range(STEPS):
        far = partner(occ, d, occ_count)
        pair_ref[d] = occ_ref[occ_index_ref[occ]] + occ_ref[occ_index_ref[far]]


def needed(blocks):
    return sorted({p for d, ps in blocks for p in ps if d > 0})


def contract(blocks, parts, first, *refs):
    refs = list(refs)
    pair_energy, row_energy, col_energy = (refs.pop(0) for _ in range(3))
    rows = [refs.pop(0), refs.pop(0)]
    near = {p: [refs.pop(0) for _ in range(parts[0, p])] for p in needed(blocks)}
    far_rows = {d: [refs.pop(0), refs.pop(0)] for d, _ in blocks if d > 0}
    far = {(d, p): [refs.pop(0) for _ in range(parts[d, p])] for d, ps in blocks for p in ps}
    sums_in = None if first else [refs.pop(0), refs.pop(0)]
    sums_out = refs
    count = rows[0].shape[0]

    def stack(parts):
        return jnp.concatenate([r[...] for r in parts], axis=0)

    own = stack(rows)
    weights = []
    for d, ps in blocks:
        direct = lax.dot_general(
            own, stack([r for p in ps for r in far[d, p]]), NT, preferred_element_type=jnp.float32
        )
        if d > 0:
            swapped = lax.dot_general(
                stack(far_rows[d]), stack([r for p in ps for r in near[p]]), NT,
                preferred_element_type=jnp.float32,
            )
        else:
            swapped = direct
        for k, p in enumerate(ps):
            cut = slice(k * count, (k + 1) * count)
            gap = pair_energy[d] - row_energy[...] - col_energy[p : p + 1, :]
            weights.append(((2.0 * direct[:, cut] - swapped[:, cut]) / gap).astype(jnp.bfloat16))
    weights = jnp.concatenate(weights, axis=1)
    columns = stack([r for d, ps in blocks for p in ps for r in far[d, p]])
    for half in range(CORES):
        part = jnp.dot(
            weights[half * count : (half + 1) * count], columns, preferred_element_type=jnp.float32
        )
        sums_out[half][...] = part if first else sums_in[half][...] + part


def finish(label, cuts, final, *refs):
    refs = list(refs)
    pair_energy, row_energy, col_energy, own, there = (refs.pop(0) for _ in range(5))
    near = [refs.pop(0) for _ in cuts]
    far = [refs.pop(0) for _ in cuts]
    count = own.shape[0]
    columns = jnp.concatenate([r[...] for r in far], axis=0)
    direct = lax.dot_general(own[...], columns, NT, preferred_element_type=jnp.float32)
    swapped = lax.dot_general(
        there[...], jnp.concatenate([r[...] for r in near], axis=0), NT,
        preferred_element_type=jnp.float32,
    )
    table = jnp.concatenate([col_energy[p : p + 1, cut] for p, cut in cuts], axis=1)
    row = jnp.concatenate([row_energy[:count, cut] for _, cut in cuts], axis=1)
    gap = pair_energy[label] - row - table
    weights = ((2.0 * direct - swapped) / gap).astype(jnp.bfloat16)
    if not final:
        sums, out = refs
        out[...] = sums[...] + jnp.dot(weights, columns, preferred_element_type=jnp.float32)
        return
    *sums, out, buffer, sems = refs
    depth = out.shape[1] // sems.shape[0]
    copies = []
    for k in range(sems.shape[0]):
        cut = slice(k * depth, (k + 1) * depth)
        part = jnp.dot(weights, columns[:, cut], preferred_element_type=jnp.float32)
        buffer[:, cut] = (sums[0][:, cut] + sums[1][:, cut]) + part
        copies.append(pltpu.make_async_copy(buffer.at[:, cut], out.at[:, cut], sems.at[k]))
        copies[-1].start()
    for copy in copies:
        copy.wait()


def per_device(aux_factors, occ_energy, vir_energy, occ_index, vir_index):
    va_count = lax.axis_size("va")
    vb_count = lax.axis_size("vb")
    occ_count = lax.axis_size("occ")
    chip_count = vb_count // CORES
    occ_rows, width, aux_width = aux_factors.shape
    assert occ_rows == 1 and vb_count % CORES == 0
    paired = occ_count == STEPS and STEPS & (STEPS - 1) == 0

    def partner(i, step, count):
        return i ^ step if paired else (i + count - step) % count

    def from_va(block, step):
        return lax.ppermute(block, "va", [((i - step) % va_count, i) for i in range(va_count)])

    def from_vb(block, step):
        move = step * CORES
        return lax.ppermute(block, "vb", [((i - move) % vb_count, i) for i in range(vb_count)])

    def from_core(block):
        return lax.ppermute(block, "vb", [(i ^ 1, i) for i in range(vb_count)])

    def from_occ(block, step):
        return lax.ppermute(
            block, "occ", [(partner(i, step, occ_count), i) for i in range(occ_count)]
        )

    own = aux_factors[0]
    line = {0: own}
    for d in range(1, STEPS):
        low = d & -d
        line[d] = from_occ(line[d - low], low)
    other = {d: from_core(line[d]) for d in range(STEPS)}
    plane_of = {(dx, dy): dx * chip_count + dy for dx in range(va_count) for dy in range(chip_count)}
    half = width // 2
    held = {}
    for d in range(STEPS):
        blocks = {"": line[d]}
        if d == 2:
            blocks = {"a": line[d][:half], "b": line[d][half:]}
        for (dx, dy), p in plane_of.items():
            if dx == 0 and dy == 0:
                held[d, p] = [line[d]]
            elif dy == 0:
                held[d, p] = [from_va(b, dx) for b in blocks.values()]
            elif dx == 0:
                held[d, p] = [from_vb(b, dy) for b in blocks.values()]
    for d in range(STEPS):
        for (dx, dy), p in plane_of.items():
            if dx > 0 and dy > 0 and d % 2 == 1:
                first, second = held[d - 1, p]
                held[d, p] = [from_occ(first, 1), from_occ(second, 1)]
            elif dx > 0 and dy > 0:
                first = held[d, plane_of[0, dy]][0]
                second = held[d, plane_of[dx, 0]][-1]
                held[d, p] = [from_va(first[:half], dx), from_vb(second[-half:], dy)]

    whole = pl.BlockSpec(memory_space=pltpu.VMEM)
    scalar = pl.BlockSpec(memory_space=pltpu.SMEM)
    f32 = jnp.float32

    def energies():
        return pl.pallas_call(
            functools.partial(prepare, (va_count, chip_count, occ_count), partner),
            out_shape=(
                jax.ShapeDtypeStruct((STEPS,), f32),
                jax.ShapeDtypeStruct((CORES * width, width), f32),
                jax.ShapeDtypeStruct((CORES * len(plane_of), width), f32),
            ),
            in_specs=[whole, scalar, scalar, scalar],
            out_specs=(scalar, whole, whole),
            cost_estimate=pl.CostEstimate(
                flops=3 * vir_index.shape[0] ** 2, bytes_accessed=1 << 18, transcendentals=0
            ),
        )(vir_index.reshape(-1, width), vir_energy, occ_index, occ_energy)

    parts = {key: len(pieces) for key, pieces in held.items()}
    tables = energies()
    total = jax.ShapeDtypeStruct((width, aux_width), f32)

    def add(blocks, sums):
        operands = [*tables, own, other[0]]
        operands += [part for p in needed(blocks) for part in held[0, p]]
        for d, _ in blocks:
            operands += [line[d], other[d]] if d > 0 else []
        operands += [part for d, ps in blocks for p in ps for part in held[d, p]]
        aliases = {}
        if sums is not None:
            aliases = {len(operands) + k: k for k in range(CORES)}
            operands += list(sums)
        count = sum(len(ps) for _, ps in blocks)
        return pl.pallas_call(
            functools.partial(contract, blocks, parts, sums is None),
            out_shape=(total, total),
            in_specs=[scalar] + [whole] * (len(operands) - 1),
            out_specs=(whole, whole),
            input_output_aliases=aliases,
            cost_estimate=pl.CostEstimate(
                flops=2 * 3 * count * CORES * width * width * aux_width,
                bytes_accessed=count * width * aux_width * 4,
                transcendentals=0,
            ),
            compiler_params=pltpu.CompilerParams(vmem_limit_bytes=24 << 20),
        )(*operands)

    here = [plane_of[0, 0]]
    xs = [p for (dx, dy), p in plane_of.items() if dx > 0 and dy == 0]
    ys = [p for (dx, dy), p in plane_of.items() if dx == 0 and dy > 0]
    cs = [p for (dx, dy), p in plane_of.items() if dx > 0 and dy > 0]
    groups = (
        ((0, here + xs + ys + cs),),
        ((1, here + xs + ys),),
        ((2, here + xs + ys),),
        ((1, cs), (2, cs), (3, here)),
        ((3, xs + ys),),
    )
    sums = None
    for blocks in groups:
        sums = add(blocks, sums)
    sums = [sums[0], from_core(sums[1])]

    pieces = parts[0, cs[0]]
    swapped = {
        (d, p, k): from_core(held[d, p][k])
        for d in (0, 3)
        for p in cs
        for k in range(pieces)
    }

    def late(k, final, *sums):
        size = width // pieces
        cut = slice(k * size, (k + 1) * size)
        operands = [*tables, own, line[3]]
        for d in (0, 3):
            operands += [held[d, p][k] for p in cs] + [swapped[d, p, k] for p in cs]
        operands += sums
        rows = [core * len(plane_of) + p for core in range(CORES) for p in cs]
        return pl.pallas_call(
            functools.partial(finish, 3, [(row, cut) for row in rows], final),
            out_shape=total,
            in_specs=[scalar] + [whole] * (len(operands) - 1),
            out_specs=pl.BlockSpec(memory_space=pl.ANY) if final else whole,
            scratch_shapes=[pltpu.VMEM(total.shape, f32), pltpu.SemaphoreType.DMA((4,))]
            if final
            else [],
            cost_estimate=pl.CostEstimate(
                flops=2 * 3 * len(rows) * width * size * aux_width,
                bytes_accessed=width * aux_width * 4,
                transcendentals=0,
            ),
            compiler_params=pltpu.CompilerParams(vmem_limit_bytes=16 << 20),
        )(*operands)

    mine = sums[0]
    for k in range(pieces - 1):
        mine = late(k, False, mine)
    return late(pieces - 1, True, mine, sums[1])[None]


def solution(mesh):
    return jax.shard_map(
        per_device,
        mesh=mesh,
        in_specs=(P("occ", ("vb", "va"), None), P(), P(), P(), P()),
        out_specs=P("occ", ("vb", "va"), None),
        check_vma=False,
    )
```

```python
import functools

import jax
import jax.numpy as jnp
from jax import lax
from jax.experimental import pallas as pl
from jax.experimental.pallas import tpu as pltpu
from jax.sharding import PartitionSpec as P


STEPS = 4
CORES = 2

NT = (((1,), (1,)), ((), ()))


def prepare(sizes, partner, index_ref, vir_ref, occ_index_ref, occ_ref, pair_ref, row_ref, col_ref):
    va_count, chip_count, occ_count = sizes
    va, vb, occ = lax.axis_index("va"), lax.axis_index("vb"), lax.axis_index("occ")
    core, chip = lax.rem(vb, CORES), vb // CORES
    index = index_ref[...]
    width = index.shape[1]

    lanes = 16
    share = vir_ref.shape[0] // lanes

    def step(k, found):
        return tuple(
            f + jnp.where(index == n * share + k, vir_ref[n * share + k], 0.0)
            for n, f in enumerate(found)
        )

    zero = jnp.zeros(index.shape, jnp.float32)
    found = lax.fori_loop(0, share, step, (zero,) * lanes, unroll=2)
    energy = sum(found[1:], found[0])

    def block(dx, dy, flip):
        other = lax.rem(chip - dy + chip_count, chip_count) * CORES + lax.rem(core + flip, CORES)
        mine = other * va_count + lax.rem(va - dx + va_count, va_count)
        picked = lax.broadcasted_iota(jnp.int32, index.shape, 0) == mine
        return jnp.sum(jnp.where(picked, energy, 0.0), axis=0, keepdims=True)

    for flip in range(CORES):
        spread = jnp.broadcast_to(block(0, 0, flip), (width, width))
        row_ref[flip * width : (flip + 1) * width, :] = jnp.transpose(spread)
    for dx in range(va_count):
        for dy in range(chip_count):
            for flip in range(CORES):
                p = (flip * va_count + dx) * chip_count + dy
                col_ref[p : p + 1, :] = block(dx, dy, flip)
    for d in range(STEPS):
        far = partner(occ, d, occ_count)
        pair = occ_ref[occ_index_ref[occ]] + occ_ref[occ_index_ref[far]]
        pair_ref[d : d + 1, :] = jnp.full((1, width), pair, jnp.float32)


def needed(blocks):
    return sorted({p for d, ps in blocks for p in ps if d > 0})


def contract(blocks, parts, first, *refs):
    refs = list(refs)
    pair_energy, row_energy, col_energy = (refs.pop(0) for _ in range(3))
    rows = [refs.pop(0), refs.pop(0)]
    near = {p: [refs.pop(0) for _ in range(parts[0, p])] for p in needed(blocks)}
    far_rows = {d: [refs.pop(0), refs.pop(0)] for d, _ in blocks if d > 0}
    far = {(d, p): [refs.pop(0) for _ in range(parts[d, p])] for d, ps in blocks for p in ps}
    sums_in = None if first else [refs.pop(0), refs.pop(0)]
    sums_out = refs
    count = rows[0].shape[0]

    def stack(parts):
        return jnp.concatenate([r[...] for r in parts], axis=0)

    own = stack(rows)
    weights = []
    for d, ps in blocks:
        direct = lax.dot_general(
            own, stack([r for p in ps for r in far[d, p]]), NT, preferred_element_type=jnp.float32
        )
        if d > 0:
            swapped = lax.dot_general(
                stack(far_rows[d]), stack([r for p in ps for r in near[p]]), NT,
                preferred_element_type=jnp.float32,
            )
        else:
            swapped = direct
        for k, p in enumerate(ps):
            cut = slice(k * count, (k + 1) * count)
            gap = pair_energy[d : d + 1, :] - row_energy[...] - col_energy[p : p + 1, :]
            weights.append(((2.0 * direct[:, cut] - swapped[:, cut]) / gap).astype(jnp.bfloat16))
    weights = jnp.concatenate(weights, axis=1)
    columns = stack([r for d, ps in blocks for p in ps for r in far[d, p]])
    for half in range(CORES):
        part = jnp.dot(
            weights[half * count : (half + 1) * count], columns, preferred_element_type=jnp.float32
        )
        sums_out[half][...] = part if first else sums_in[half][...] + part


def finish(label, cuts, final, *refs):
    refs = list(refs)
    pair_energy, row_energy, col_energy, own, there = (refs.pop(0) for _ in range(5))
    near = [refs.pop(0) for _ in cuts]
    far = [refs.pop(0) for _ in cuts]
    count = own.shape[0]
    columns = jnp.concatenate([r[...] for r in far], axis=0)
    direct = lax.dot_general(own[...], columns, NT, preferred_element_type=jnp.float32)
    swapped = lax.dot_general(
        there[...], jnp.concatenate([r[...] for r in near], axis=0), NT,
        preferred_element_type=jnp.float32,
    )
    table = jnp.concatenate([col_energy[p : p + 1, cut] for p, cut in cuts], axis=1)
    row = jnp.concatenate([row_energy[:count, cut] for _, cut in cuts], axis=1)
    pair = jnp.concatenate([pair_energy[label : label + 1, cut] for _, cut in cuts], axis=1)
    gap = pair - row - table
    weights = ((2.0 * direct - swapped) / gap).astype(jnp.bfloat16)
    if not final:
        sums, out = refs
        out[...] = sums[...] + jnp.dot(weights, columns, preferred_element_type=jnp.float32)
        return
    *sums, out, buffer, sems = refs
    depth = out.shape[1] // sems.shape[0]
    copies = []
    for k in range(sems.shape[0]):
        cut = slice(k * depth, (k + 1) * depth)
        part = jnp.dot(weights, columns[:, cut], preferred_element_type=jnp.float32)
        buffer[:, cut] = (sums[0][:, cut] + sums[1][:, cut]) + part
        copies.append(pltpu.make_async_copy(buffer.at[:, cut], out.at[:, cut], sems.at[k]))
        copies[-1].start()
    for copy in copies:
        copy.wait()


def per_device(aux_factors, occ_energy, vir_energy, occ_index, vir_index):
    va_count = lax.axis_size("va")
    vb_count = lax.axis_size("vb")
    occ_count = lax.axis_size("occ")
    chip_count = vb_count // CORES
    occ_rows, width, aux_width = aux_factors.shape
    assert occ_rows == 1 and vb_count % CORES == 0
    paired = occ_count == STEPS and STEPS & (STEPS - 1) == 0

    def partner(i, step, count):
        return i ^ step if paired else (i + count - step) % count

    def from_va(block, step):
        return lax.ppermute(block, "va", [((i - step) % va_count, i) for i in range(va_count)])

    def from_vb(block, step):
        move = step * CORES
        return lax.ppermute(block, "vb", [((i - move) % vb_count, i) for i in range(vb_count)])

    def from_core(block):
        return lax.ppermute(block, "vb", [(i ^ 1, i) for i in range(vb_count)])

    def from_occ(block, step):
        return lax.ppermute(
            block, "occ", [(partner(i, step, occ_count), i) for i in range(occ_count)]
        )

    own = aux_factors[0]
    line = {0: own}
    for d in range(1, STEPS):
        low = d & -d
        line[d] = from_occ(line[d - low], low)
    other = {d: from_core(line[d]) for d in range(STEPS)}
    plane_of = {(dx, dy): dx * chip_count + dy for dx in range(va_count) for dy in range(chip_count)}
    half = width // 2
    held = {}
    for d in range(STEPS):
        blocks = {"": line[d]}
        if d == 2:
            blocks = {"a": line[d][:half], "b": line[d][half:]}
        for (dx, dy), p in plane_of.items():
            if dx == 0 and dy == 0:
                held[d, p] = [line[d]]
            elif dy == 0:
                held[d, p] = [from_va(b, dx) for b in blocks.values()]
            elif dx == 0:
                held[d, p] = [from_vb(b, dy) for b in blocks.values()]
    for d in range(STEPS):
        for (dx, dy), p in plane_of.items():
            if dx > 0 and dy > 0 and d % 2 == 1:
                first, second = held[d - 1, p]
                held[d, p] = [from_occ(first, 1), from_occ(second, 1)]
            elif dx > 0 and dy > 0:
                first = held[d, plane_of[0, dy]][0]
                second = held[d, plane_of[dx, 0]][-1]
                held[d, p] = [from_va(first[:half], dx), from_vb(second[-half:], dy)]

    whole = pl.BlockSpec(memory_space=pltpu.VMEM)
    scalar = pl.BlockSpec(memory_space=pltpu.SMEM)
    f32 = jnp.float32

    def energies():
        return pl.pallas_call(
            functools.partial(prepare, (va_count, chip_count, occ_count), partner),
            out_shape=(
                jax.ShapeDtypeStruct((STEPS, width), f32),
                jax.ShapeDtypeStruct((CORES * width, width), f32),
                jax.ShapeDtypeStruct((CORES * len(plane_of), width), f32),
            ),
            in_specs=[whole, scalar, scalar, scalar],
            out_specs=(whole, whole, whole),
            cost_estimate=pl.CostEstimate(
                flops=3 * vir_index.shape[0] ** 2, bytes_accessed=1 << 18, transcendentals=0
            ),
        )(vir_index.reshape(-1, width), vir_energy, occ_index, occ_energy)

    parts = {key: len(pieces) for key, pieces in held.items()}
    tables = energies()
    total = jax.ShapeDtypeStruct((width, aux_width), f32)

    def add(blocks, sums):
        operands = [*tables, own, other[0]]
        operands += [part for p in needed(blocks) for part in held[0, p]]
        for d, _ in blocks:
            operands += [line[d], other[d]] if d > 0 else []
        operands += [part for d, ps in blocks for p in ps for part in held[d, p]]
        aliases = {}
        if sums is not None:
            aliases = {len(operands) + k: k for k in range(CORES)}
            operands += list(sums)
        count = sum(len(ps) for _, ps in blocks)
        return pl.pallas_call(
            functools.partial(contract, blocks, parts, sums is None),
            out_shape=(total, total),
            in_specs=[whole] * len(operands),
            out_specs=(whole, whole),
            input_output_aliases=aliases,
            cost_estimate=pl.CostEstimate(
                flops=2 * 3 * count * CORES * width * width * aux_width,
                bytes_accessed=count * width * aux_width * 4,
                transcendentals=0,
            ),
            compiler_params=pltpu.CompilerParams(vmem_limit_bytes=24 << 20),
        )(*operands)

    here = [plane_of[0, 0]]
    xs = [p for (dx, dy), p in plane_of.items() if dx > 0 and dy == 0]
    ys = [p for (dx, dy), p in plane_of.items() if dx == 0 and dy > 0]
    cs = [p for (dx, dy), p in plane_of.items() if dx > 0 and dy > 0]
    groups = (
        ((0, here + xs + ys + cs),),
        ((1, here + xs + ys),),
        ((2, here + xs + ys),),
        ((1, cs), (2, cs), (3, here)),
        ((3, xs + ys),),
    )
    sums = None
    for blocks in groups:
        sums = add(blocks, sums)
    sums = [sums[0], from_core(sums[1])]

    pieces = parts[0, cs[0]]
    swapped = {
        (d, p, k): from_core(held[d, p][k])
        for d in (0, 3)
        for p in cs
        for k in range(pieces)
    }

    def late(k, final, *sums):
        size = width // pieces
        cut = slice(k * size, (k + 1) * size)
        operands = [*tables, own, line[3]]
        for d in (0, 3):
            operands += [held[d, p][k] for p in cs] + [swapped[d, p, k] for p in cs]
        operands += sums
        rows = [core * len(plane_of) + p for core in range(CORES) for p in cs]
        return pl.pallas_call(
            functools.partial(finish, 3, [(row, cut) for row in rows], final),
            out_shape=total,
            in_specs=[whole] * len(operands),
            out_specs=pl.BlockSpec(memory_space=pl.ANY) if final else whole,
            scratch_shapes=[pltpu.VMEM(total.shape, f32), pltpu.SemaphoreType.DMA((4,))]
            if final
            else [],
            cost_estimate=pl.CostEstimate(
                flops=2 * 3 * len(rows) * width * size * aux_width,
                bytes_accessed=width * aux_width * 4,
                transcendentals=0,
            ),
            compiler_params=pltpu.CompilerParams(vmem_limit_bytes=16 << 20),
        )(*operands)

    mine = sums[0]
    for k in range(pieces - 1):
        mine = late(k, False, mine)
    return late(pieces - 1, True, mine, sums[1])[None]


def solution(mesh):
    return jax.shard_map(
        per_device,
        mesh=mesh,
        in_specs=(P("occ", ("vb", "va"), None), P(), P(), P(), P()),
        out_specs=P("occ", ("vb", "va"), None),
        check_vma=False,
    )
```

```python
import functools

import jax
import jax.numpy as jnp
from jax import lax
from jax.experimental import pallas as pl
from jax.experimental.pallas import tpu as pltpu
from jax.sharding import PartitionSpec as P


STEPS = 4
CORES = 2

NT = (((1,), (1,)), ((), ()))


def prepare(sizes, partner, index_ref, vir_ref, occ_index_ref, occ_ref, pair_ref, row_ref, col_ref):
    va_count, chip_count, occ_count = sizes
    va, vb, occ = lax.axis_index("va"), lax.axis_index("vb"), lax.axis_index("occ")
    core, chip = lax.rem(vb, CORES), vb // CORES
    index = index_ref[...]
    width = index.shape[1]

    lanes = 16
    share = vir_ref.shape[0] // lanes

    def step(k, found):
        return tuple(
            f + jnp.where(index == n * share + k, vir_ref[n * share + k], 0.0)
            for n, f in enumerate(found)
        )

    zero = jnp.zeros(index.shape, jnp.float32)
    found = lax.fori_loop(0, share, step, (zero,) * lanes, unroll=2)
    energy = sum(found[1:], found[0])

    def block(dx, dy, flip):
        other = lax.rem(chip - dy + chip_count, chip_count) * CORES + lax.rem(core + flip, CORES)
        mine = other * va_count + lax.rem(va - dx + va_count, va_count)
        picked = lax.broadcasted_iota(jnp.int32, index.shape, 0) == mine
        return jnp.sum(jnp.where(picked, energy, 0.0), axis=0, keepdims=True)

    for flip in range(CORES):
        spread = jnp.broadcast_to(block(0, 0, flip), (width, width))
        row_ref[flip * width : (flip + 1) * width, :] = jnp.transpose(spread)
    for dx in range(va_count):
        for dy in range(chip_count):
            for flip in range(CORES):
                p = (flip * va_count + dx) * chip_count + dy
                col_ref[p : p + 1, :] = block(dx, dy, flip)
    for d in range(STEPS):
        far = partner(occ, d, occ_count)
        pair = occ_ref[occ_index_ref[occ]] + occ_ref[occ_index_ref[far]]
        pair_ref[d : d + 1, :] = jnp.full((1, width), pair, jnp.float32)


def needed(blocks):
    return sorted({p for d, ps in blocks for p in ps if d > 0})


def contract(blocks, parts, first, halves, *refs):
    refs = list(refs)
    pair_energy, row_energy, col_energy = (refs.pop(0) for _ in range(3))
    rows = [refs.pop(0) for _ in halves]
    near = {p: [refs.pop(0) for _ in range(parts[0, p])] for p in needed(blocks)}
    far_rows = {d: [refs.pop(0) for _ in halves] for d, _ in blocks if d > 0}
    far = {(d, p): [refs.pop(0) for _ in range(parts[d, p])] for d, ps in blocks for p in ps}
    sums_in = None if first else [refs.pop(0) for _ in halves]
    sums_out = refs
    count = rows[0].shape[0]

    def stack(parts):
        return jnp.concatenate([r[...] for r in parts], axis=0)

    own = stack(rows)
    row = row_energy[halves[0] * count : (halves[-1] + 1) * count, :]
    weights = []
    for d, ps in blocks:
        direct = lax.dot_general(
            own, stack([r for p in ps for r in far[d, p]]), NT, preferred_element_type=jnp.float32
        )
        if d > 0:
            swapped = lax.dot_general(
                stack(far_rows[d]), stack([r for p in ps for r in near[p]]), NT,
                preferred_element_type=jnp.float32,
            )
        else:
            swapped = direct
        for k, p in enumerate(ps):
            cut = slice(k * count, (k + 1) * count)
            gap = pair_energy[d : d + 1, :] - row - col_energy[p : p + 1, :]
            weights.append(((2.0 * direct[:, cut] - swapped[:, cut]) / gap).astype(jnp.bfloat16))
    weights = jnp.concatenate(weights, axis=1)
    columns = stack([r for d, ps in blocks for p in ps for r in far[d, p]])
    for half in range(len(halves)):
        part = jnp.dot(
            weights[half * count : (half + 1) * count], columns, preferred_element_type=jnp.float32
        )
        sums_out[half][...] = part if first else sums_in[half][...] + part


def finish(label, cuts, final, *refs):
    refs = list(refs)
    pair_energy, row_energy, col_energy, own, there = (refs.pop(0) for _ in range(5))
    near = [refs.pop(0) for _ in cuts]
    far = [refs.pop(0) for _ in cuts]
    count = own.shape[0]
    columns = jnp.concatenate([r[...] for r in far], axis=0)
    direct = lax.dot_general(own[...], columns, NT, preferred_element_type=jnp.float32)
    swapped = lax.dot_general(
        there[...], jnp.concatenate([r[...] for r in near], axis=0), NT,
        preferred_element_type=jnp.float32,
    )
    table = jnp.concatenate([col_energy[p : p + 1, cut] for p, cut in cuts], axis=1)
    row = jnp.concatenate([row_energy[:count, cut] for _, cut in cuts], axis=1)
    pair = jnp.concatenate([pair_energy[label : label + 1, cut] for _, cut in cuts], axis=1)
    gap = pair - row - table
    weights = ((2.0 * direct - swapped) / gap).astype(jnp.bfloat16)
    if not final:
        sums, out = refs
        out[...] = sums[...] + jnp.dot(weights, columns, preferred_element_type=jnp.float32)
        return
    *sums, out, buffer, sems = refs
    depth = out.shape[1] // sems.shape[0]
    copies = []
    for k in range(sems.shape[0]):
        cut = slice(k * depth, (k + 1) * depth)
        part = jnp.dot(weights, columns[:, cut], preferred_element_type=jnp.float32)
        buffer[:, cut] = (sums[0][:, cut] + sums[1][:, cut]) + part
        copies.append(pltpu.make_async_copy(buffer.at[:, cut], out.at[:, cut], sems.at[k]))
        copies[-1].start()
    for copy in copies:
        copy.wait()


def per_device(aux_factors, occ_energy, vir_energy, occ_index, vir_index):
    va_count = lax.axis_size("va")
    vb_count = lax.axis_size("vb")
    occ_count = lax.axis_size("occ")
    chip_count = vb_count // CORES
    occ_rows, width, aux_width = aux_factors.shape
    assert occ_rows == 1 and vb_count % CORES == 0
    paired = occ_count == STEPS and STEPS & (STEPS - 1) == 0

    def partner(i, step, count):
        return i ^ step if paired else (i + count - step) % count

    def from_va(block, step):
        return lax.ppermute(block, "va", [((i - step) % va_count, i) for i in range(va_count)])

    def from_vb(block, step):
        move = step * CORES
        return lax.ppermute(block, "vb", [((i - move) % vb_count, i) for i in range(vb_count)])

    def from_core(block):
        return lax.ppermute(block, "vb", [(i ^ 1, i) for i in range(vb_count)])

    def from_occ(block, step):
        return lax.ppermute(
            block, "occ", [(partner(i, step, occ_count), i) for i in range(occ_count)]
        )

    own = aux_factors[0]
    line = {0: own}
    for d in range(1, STEPS):
        low = d & -d
        line[d] = from_occ(line[d - low], low)
    other = {d: from_core(line[d]) for d in range(STEPS)}
    plane_of = {(dx, dy): dx * chip_count + dy for dx in range(va_count) for dy in range(chip_count)}
    half = width // 2
    held = {}
    for d in range(STEPS):
        blocks = {"": line[d]}
        if d == 2:
            blocks = {"a": line[d][:half], "b": line[d][half:]}
        for (dx, dy), p in plane_of.items():
            if dx == 0 and dy == 0:
                held[d, p] = [line[d]]
            elif dy == 0:
                held[d, p] = [from_va(b, dx) for b in blocks.values()]
            elif dx == 0:
                held[d, p] = [from_vb(b, dy) for b in blocks.values()]
    for d in range(STEPS):
        for (dx, dy), p in plane_of.items():
            if dx > 0 and dy > 0 and d % 2 == 1:
                first, second = held[d - 1, p]
                held[d, p] = [from_occ(first, 1), from_occ(second, 1)]
            elif dx > 0 and dy > 0:
                first = held[d, plane_of[0, dy]][0]
                second = held[d, plane_of[dx, 0]][-1]
                held[d, p] = [from_va(first[:half], dx), from_vb(second[-half:], dy)]

    whole = pl.BlockSpec(memory_space=pltpu.VMEM)
    scalar = pl.BlockSpec(memory_space=pltpu.SMEM)
    f32 = jnp.float32

    def energies():
        return pl.pallas_call(
            functools.partial(prepare, (va_count, chip_count, occ_count), partner),
            out_shape=(
                jax.ShapeDtypeStruct((STEPS, width), f32),
                jax.ShapeDtypeStruct((CORES * width, width), f32),
                jax.ShapeDtypeStruct((CORES * len(plane_of), width), f32),
            ),
            in_specs=[whole, scalar, scalar, scalar],
            out_specs=(whole, whole, whole),
            cost_estimate=pl.CostEstimate(
                flops=3 * vir_index.shape[0] ** 2, bytes_accessed=1 << 18, transcendentals=0
            ),
        )(vir_index.reshape(-1, width), vir_energy, occ_index, occ_energy)

    parts = {key: len(pieces) for key, pieces in held.items()}
    tables = energies()
    total = jax.ShapeDtypeStruct((width, aux_width), f32)

    def add(blocks, sums, halves=tuple(range(CORES))):
        operands = [*tables, *[(own, other[0])[h] for h in halves]]
        operands += [part for p in needed(blocks) for part in held[0, p]]
        for d, _ in blocks:
            operands += [(line[d], other[d])[h] for h in halves] if d > 0 else []
        operands += [part for d, ps in blocks for p in ps for part in held[d, p]]
        aliases = {}
        if sums is not None:
            aliases = {len(operands) + k: k for k in range(len(halves))}
            operands += list(sums)
        count = sum(len(ps) for _, ps in blocks)
        return pl.pallas_call(
            functools.partial(contract, blocks, parts, sums is None, halves),
            out_shape=(total,) * len(halves),
            in_specs=[whole] * len(operands),
            out_specs=(whole,) * len(halves),
            input_output_aliases=aliases,
            cost_estimate=pl.CostEstimate(
                flops=2 * 3 * count * len(halves) * width * width * aux_width,
                bytes_accessed=count * width * aux_width * 4,
                transcendentals=0,
            ),
            compiler_params=pltpu.CompilerParams(vmem_limit_bytes=24 << 20),
        )(*operands)

    here = [plane_of[0, 0]]
    xs = [p for (dx, dy), p in plane_of.items() if dx > 0 and dy == 0]
    ys = [p for (dx, dy), p in plane_of.items() if dx == 0 and dy > 0]
    cs = [p for (dx, dy), p in plane_of.items() if dx > 0 and dy > 0]
    groups = (
        ((0, here + xs + ys + cs),),
        ((1, here + xs + ys),),
        ((2, here + xs + ys),),
        ((1, cs), (2, cs), (3, here)),
        ((3, xs + ys),),
    )
    sums = None
    for blocks in groups[:-1]:
        sums = add(blocks, sums)
    (away,) = add(groups[-1], sums[1:], (1,))
    (kept,) = add(groups[-1], sums[:1], (0,))
    sums = [kept, away]
    sums = [sums[0], from_core(sums[1])]

    pieces = parts[0, cs[0]]
    swapped = {
        (d, p, k): from_core(held[d, p][k])
        for d in (0, 3)
        for p in cs
        for k in range(pieces)
    }

    def late(k, final, *sums):
        size = width // pieces
        cut = slice(k * size, (k + 1) * size)
        operands = [*tables, own, line[3]]
        for d in (0, 3):
            operands += [held[d, p][k] for p in cs] + [swapped[d, p, k] for p in cs]
        operands += sums
        rows = [core * len(plane_of) + p for core in range(CORES) for p in cs]
        return pl.pallas_call(
            functools.partial(finish, 3, [(row, cut) for row in rows], final),
            out_shape=total,
            in_specs=[whole] * len(operands),
            out_specs=pl.BlockSpec(memory_space=pl.ANY) if final else whole,
            scratch_shapes=[pltpu.VMEM(total.shape, f32), pltpu.SemaphoreType.DMA((4,))]
            if final
            else [],
            cost_estimate=pl.CostEstimate(
                flops=2 * 3 * len(rows) * width * size * aux_width,
                bytes_accessed=width * aux_width * 4,
                transcendentals=0,
            ),
            compiler_params=pltpu.CompilerParams(vmem_limit_bytes=16 << 20),
        )(*operands)

    mine = sums[0]
    for k in range(pieces - 1):
        mine = late(k, False, mine)
    return late(pieces - 1, True, mine, sums[1])[None]


def solution(mesh):
    return jax.shard_map(
        per_device,
        mesh=mesh,
        in_specs=(P("occ", ("vb", "va"), None), P(), P(), P(), P()),
        out_specs=P("occ", ("vb", "va"), None),
        check_vma=False,
    )
```
